32 devices in a mesh: group: 4 (over x, core), inner: 8 (over z, y).
Axes of the slice: x: 2, y: 2, z: 4, core: 2. Of those that a mesh axis runs over, the one named last changes fastest.
Arguments:
- tokens: bfloat16 [2, 2048, 2048], P(None, ('group', 'inner')), may hold values from -6 to 6
- route_weight: float32 [2, 2048, 6], P(None, ('group', 'inner')), may hold values from 0.05 to 0.5
- routes: int32 [2, 2048, 6], P(None, ('group', 'inner')), may hold values from 0 to 63, all different within a row; in each aligned block of 64 rows (0 to 63, 64 to 127, ..., all dimensions but the last counted through in order) at most 6 rows name the same one
- replica: int32 [2, 2048, 6], P(None, ('group', 'inner')), may hold values from 0 to 1
- old_place: int32 [128], replicated, may hold values from 0 to 63, as said below
- new_src: int32 [128], replicated, may hold values from 0 to 127, as said below
- w_in: bfloat16 [128, 2816, 2048], P(('group', 'inner')), may hold values from -0.125 to 0.125
- w_out: bfloat16 [128, 1408, 2048], P(('group', 'inner')), may hold values from -0.15625 to 0.15625
- queries: bfloat16 [2, 32, 16, 576], P(None, 'group'), may hold values from -21 to 21
- latent_cache: bfloat16 [2, 384, 256, 576], P(None, ('group', 'inner')), may hold values from -6 to 6
- block_req: int32 [2, 384], P(None, ('group', 'inner')), may hold values from 0 to 7, as said below
- block_len: int32 [2, 384], P(None, ('group', 'inner')), may hold values from 0 to 256
Outputs:
- moe_out: bfloat16 [2, 2048, 2048], P(None, ('group', 'inner'))
- attention: bfloat16 [2, 32, 16, 512], P(None, 'group')
The draws below stay inside these ranges and needn't reach their ends.
Inputs may be any that keep to these rules, and one draw needn't show every extreme that they name: `routes`: within one batch, in each aligned block of 64 tokens (the tokens of one device) no expert is named by more than 6 tokens; a token names 6 different experts. `old_place`: every expert holds exactly two slots. old_place[new_src] names every expert exactly twice. `block_req`: in each batch and group one request has exactly 8192 positions and the others 1024 to 2048; a request's positions fill whole blocks except its last; blocks with block_len 0 are unused.
All inputs are finite; a program needn't handle non-finite values.
Results may differ from the reference program's by a relative error of at most 0.014.
Values may be sent and summed in bfloat16 or wider, within the bound.
A program may use at most 256 MiB of HBM per device.

```python
import math
import jax
import jax.numpy as jnp
import numpy as np
from jax import lax

D = 2048
FF = 1408
EXPERTS = 64
TOPK = 6
H = 16
LAT = 512
KDIM = 576
SLOTS = 128
TOK_DEV = 64
MOST = 6
TOKENS = 2048
REQ_GROUP = 8
REQS = 32
SPAN = 256
MAXLEN = 8192
LMIN = 1024
LMID = 2048
CH_GROUP = 96
N_GROUP = 4


def place_tables(key):
    base_list = jnp.arange(SLOTS, dtype=jnp.int32) % EXPERTS
    old_place = jax.random.permutation(jax.random.fold_in(key, 101), base_list)
    new_expert = jax.random.permutation(jax.random.fold_in(key, 102), base_list)
    choose_copy = jax.random.randint(jax.random.fold_in(key, 103), (SLOTS,), 0, 2)
    slot_hits = (old_place[:, None] == jnp.arange(EXPERTS, dtype=jnp.int32)[None, :]).astype(jnp.int32)
    replica_rank = jnp.sum((jnp.cumsum(slot_hits, axis=0) - slot_hits) * slot_hits, axis=1)
    matches = (old_place[None, :] == new_expert[:, None]) & (replica_rank[None, :] == choose_copy[:, None])
    new_src = jnp.sum(jnp.where(matches, jnp.arange(SLOTS, dtype=jnp.int32)[None, :], 0), axis=1)
    return (old_place.astype(jnp.int32), new_src.astype(jnp.int32))


def draw_old_place(key, part):
    return place_tables(key)[0]


def draw_new_src(key, part):
    return place_tables(key)[1]


def group_layout(key):
    lengths = jax.random.randint(jax.random.fold_in(key, 1), (REQ_GROUP,), LMIN, LMID + 1)
    longest = jax.random.randint(jax.random.fold_in(key, 2), (), 0, REQ_GROUP)
    lengths = jnp.where(jnp.arange(REQ_GROUP) == longest, MAXLEN, lengths)
    blocks_of = (lengths + SPAN - 1) // SPAN
    end_block = jnp.cumsum(blocks_of)
    start_block = end_block - blocks_of
    indices = jnp.arange(CH_GROUP)
    owner_req = jnp.sum((indices[:, None] >= end_block[None, :]).astype(jnp.int32), axis=1)
    is_used = owner_req < REQ_GROUP
    owner_req = jnp.minimum(owner_req, REQ_GROUP - 1)
    own_onehot = owner_req[:, None] == jnp.arange(REQ_GROUP)[None, :]
    own_start = jnp.sum(jnp.where(own_onehot, start_block[None, :], 0), axis=1)
    own_length = jnp.sum(jnp.where(own_onehot, lengths[None, :], 0), axis=1)
    filled = jnp.where(is_used, jnp.clip(own_length - (indices - own_start) * SPAN, 0, SPAN), 0)
    shuffle = jax.random.permutation(jax.random.fold_in(key, 3), CH_GROUP)
    req_table = jnp.zeros((CH_GROUP,), jnp.int32).at[shuffle].set(jnp.where(is_used, owner_req, 0).astype(jnp.int32))
    len_table = jnp.zeros((CH_GROUP,), jnp.int32).at[shuffle].set(filled.astype(jnp.int32))
    first_block = jnp.sum(jnp.where(indices[None, :] == start_block[:, None], shuffle[None, :], 0), axis=1)
    return (req_table, len_table, first_block.astype(jnp.int32))


def cache_layout(key):
    group_keys = jax.random.split(jax.random.fold_in(key, 17), 2 * N_GROUP)
    return jax.vmap(group_layout)(group_keys)


def draw_block_req(key, part):
    return cache_layout(key)[0].reshape(2, N_GROUP * CH_GROUP)


def draw_block_len(key, part):
    return cache_layout(key)[1].reshape(2, N_GROUP * CH_GROUP)


def draw_latent_cache(key, part):
    base_draw = jnp.clip(jax.random.normal(jax.random.fold_in(key, 41), (2, N_GROUP * CH_GROUP, SPAN, KDIM), jnp.float32), -6.0, 6.0)
    return base_draw.astype(jnp.bfloat16)


def draw_queries(key, part):
    base_draw = jnp.clip(0.6 * jax.random.normal(jax.random.fold_in(key, 43), (2, N_GROUP, REQ_GROUP, H, KDIM), jnp.float32), -3.0, 3.0)
    return base_draw.reshape(2, N_GROUP * REQ_GROUP, H, KDIM).astype(jnp.bfloat16)


def set_ends(result, rng, low, high):
    place = [jax.random.randint(jax.random.fold_in(rng, axis), (), 0, length) for axis, length in enumerate(result.shape)]
    widest = result.shape.index(max(result.shape))
    beside = place[:widest] + [(place[widest] + 1) % result.shape[widest]] + place[widest + 1:]
    return result.at[tuple(place)].set(low).at[tuple(beside)].set(high)


def steps_of(rng, extent, cuts, low, top_value):
    loudness, own = 1.0, jax.random.fold_in(rng, 6)
    for axis_at, blocks in cuts:
        heights = jnp.exp(jax.random.uniform(jax.random.fold_in(own, axis_at), (blocks,), jnp.float32, low / len(cuts), top_value / len(cuts)))
        loudness = loudness * jnp.repeat(heights, extent[axis_at] // blocks).reshape([-1 if axis == axis_at else 1 for axis in range(len(extent))])
    return loudness


def routed_block(own_key, own, number, rows, number_of, top, bound, skew):
    order = jax.random.permutation(own_key, number_of)
    packed, common = portions_of(number_of, rows * top, bound, skew, True), portions_of(number_of, rows * top, bound, skew, False)
    places = jnp.arange(number_of)

    def named(sizes, rotation):
        used = int((sizes > 0).sum())
        fixed = max(1, used // 4)
        shifted = fixed + (places - fixed + rotation * (used - fixed)) % max(1, number_of - fixed)
        return jnp.zeros((number_of,), jnp.int32).at[order[jnp.where(places < fixed, places, shifted)]].set(jnp.asarray(sizes, jnp.int32))

    sizes = jnp.where(number % 4 == 0, named(packed, number // 4), named(common, number - number // 4 - 1))
    mixed = jax.random.permutation(jax.random.fold_in(own, 3), number_of)
    donor, receiver = mixed[0:number_of // 2 * 2:2], mixed[1:number_of // 2 * 2:2]
    margin = jnp.minimum(sizes[donor] - 1, bound - sizes[receiver]) // 2
    margin = jnp.where((donor == order[0]) | (receiver == order[0]) | (sizes[receiver] == 0), 0, jnp.maximum(margin, 0))
    shifted = jax.random.randint(jax.random.fold_in(own, 4), (number_of // 2,), 0, 1 << 20) % (margin + 1)
    sizes = sizes.at[donor].add(-shifted).at[receiver].add(shifted)
    labels = jnp.searchsorted(jnp.cumsum(sizes), jnp.arange(rows * top), side="right").astype(jnp.int32)
    table = labels.reshape(top, rows).T
    table = table[jax.random.permutation(jax.random.fold_in(own, 1), rows)]
    rotation = jax.random.randint(jax.random.fold_in(own, 2), (rows, 1), 0, top)
    return jnp.take_along_axis(table, (jnp.arange(top)[None, :] + rotation) % top, axis=1)


def portions_of(count, total, bound, lean, full):
    portions = [(1 << 20) // math.isqrt(grade ** lean) + 1 for grade in range(1, count + 1)]
    largest = bound if full else min(bound, max(-(-total // count), total * portions[0] // sum(portions)))
    least = 1 if total - largest >= count - 1 else 0
    given, spare = [largest] + [least] * (count - 1), total - largest - least * (count - 1)
    while spare > 0:
        free = [i for i in range(1, count) if given[i] < largest] or [i for i in range(1, count) if given[i] < bound]
        mass, left = sum([portions[i] for i in free]), spare
        for i in free:
            more = min(bound - given[i], max(1, left * portions[i] // mass), spare)
            given[i] = given[i] + more
            spare = spare - more
    return np.array(given)


def noise(stream_key, shape, spread, reach, cuts=(), kind=jnp.bfloat16):
    factor_of = steps_of(stream_key, shape, cuts, -0.22, 0.18) if cuts else 1.0
    values = jax.random.normal(stream_key, shape, jnp.float32) * spread * factor_of
    return jnp.minimum(jnp.maximum(values, -reach), reach).astype(kind)


def setup_inputs(seed: int = 0) -> dict:
    key_of = jax.random.split(jax.random.key(seed), 13)
    tokens = noise(key_of[0], (2, TOKENS, D), 1.0, 6.0, ((1, 32),))
    route_weight = jnp.clip(jnp.exp(math.log(0.5) - 2.3025851 * jax.random.uniform(key_of[1], (2, TOKENS, TOPK), jnp.float32) ** steps_of(key_of[1], (2, TOKENS, TOPK), ((1, 32),), -0.2, 0.2)), 0.05, 0.5)
    routes_keys = jax.random.split(jax.random.fold_in(key_of[2], 1), 2 * TOKENS // TOK_DEV)
    routes_turns = jax.random.permutation(jax.random.fold_in(key_of[2], 3), 2 * TOKENS // TOK_DEV)
    routes = jax.vmap(lambda own, number: routed_block(jax.random.fold_in(key_of[2], 2), own, number, TOK_DEV, EXPERTS, TOPK, MOST, 2))(routes_keys, routes_turns).reshape((2, TOKENS, TOPK))
    replica = set_ends(jax.random.randint(key_of[3], (2, TOKENS, TOPK), 0, 2), jax.random.fold_in(key_of[3], 1), 0, 1).astype(jnp.int32)
    old_place = draw_old_place(jax.random.fold_in(key_of[12], 71), 0)
    new_src = draw_new_src(jax.random.fold_in(key_of[12], 71), 0)
    w_in = noise(key_of[6], (SLOTS, 2 * FF, D), D ** -0.5, 0.125, ((0, 32),))
    w_out = noise(key_of[7], (SLOTS, FF, D), FF ** -0.5, 0.15625, ((0, 32),))
    queries = draw_queries(jax.random.fold_in(key_of[12], 71), 0)
    latent_cache = draw_latent_cache(jax.random.fold_in(key_of[12], 71), 0)
    block_req = draw_block_req(jax.random.fold_in(key_of[12], 71), 0)
    block_len = draw_block_len(jax.random.fold_in(key_of[12], 71), 0)
    return dict(tokens=tokens, route_weight=route_weight, routes=routes, replica=replica, old_place=old_place, new_src=new_src, w_in=w_in, w_out=w_out, queries=queries, latent_cache=latent_cache, block_req=block_req, block_len=block_len)


score_scale = 192.0 ** -0.5
floor_value = -1.0e30
block_rows = 64


def block_attention(queries, latent_cache, block_req, block_len, latent):
    requests, head_count, feat_width = queries.shape
    blocks, cache_rows, _ = latent_cache.shape
    belongs = block_req[:, None] == jnp.arange(requests, dtype=jnp.int32)[None, :]
    chosen = jnp.dot(belongs.astype(jnp.bfloat16), queries.reshape(requests, head_count * feat_width), preferred_element_type=jnp.float32)
    chosen = chosen.astype(jnp.bfloat16).reshape(blocks, head_count, feat_width)
    scores = jnp.einsum("chk,cpk->chp", chosen.astype(jnp.float32), latent_cache.astype(jnp.float32)) * score_scale
    live_rows = jnp.arange(cache_rows, dtype=jnp.int32)[None, :] < block_len[:, None]
    scores = jnp.where(live_rows[:, None, :], scores, floor_value)
    block_max = jnp.max(scores, axis=2)
    req_max = jnp.max(jnp.where(belongs[:, :, None], block_max[:, None, :], floor_value), axis=0)
    own_max = jnp.sum(jnp.where(belongs[:, :, None], req_max[None, :, :], 0.0), axis=1)
    exp_scores = jnp.where(live_rows[:, None, :], jnp.exp(scores - own_max[:, :, None]), 0.0)
    block_total = jnp.sum(exp_scores, axis=2)
    weights = exp_scores.astype(jnp.bfloat16)
    block_out = jnp.einsum("chp,cpl->chl", weights.astype(jnp.float32), latent_cache[:, :, :latent].astype(jnp.float32))
    belongs_f = belongs.astype(jnp.float32)
    req_total = jnp.einsum("cr,ch->rh", belongs_f, block_total, precision=lax.Precision.HIGHEST)
    req_out = jnp.einsum("cr,chl->rhl", belongs_f, block_out, precision=lax.Precision.HIGHEST)
    return req_max, req_total, req_out


def slot_of_route(expert_of_slot, routes, replica):
    slot_count = expert_of_slot.shape[0]
    slot_hits = (expert_of_slot[:, None] == jnp.arange(EXPERTS, dtype=jnp.int32)[None, :]).astype(jnp.int32)
    replica_rank = jnp.sum((jnp.cumsum(slot_hits, axis=0) - slot_hits) * slot_hits, axis=1)
    flat_expert = routes.reshape(-1)
    flat_replica = replica.reshape(-1)
    matches = (expert_of_slot[None, :] == flat_expert[:, None]) & (replica_rank[None, :] == flat_replica[:, None])
    return jnp.sum(jnp.where(matches, jnp.arange(slot_count, dtype=jnp.int32)[None, :], 0), axis=1).astype(jnp.int32)


def moe_reference(tokens, route_weight, target, w_in, w_out):
    row_total = target.shape[0]
    feat_width = tokens.shape[1]
    token_rows = jnp.repeat(tokens, TOPK, axis=0)
    sorted_idx = jnp.argsort(target, stable=True).astype(jnp.int32)
    ordered = jnp.concatenate([token_rows[sorted_idx], jnp.zeros((block_rows, feat_width), token_rows.dtype)])
    counts = jnp.sum((target[:, None] == jnp.arange(SLOTS, dtype=jnp.int32)[None, :]).astype(jnp.int32), axis=0).astype(jnp.int32)
    starts = (jnp.cumsum(counts) - counts).astype(jnp.int32)

    def per_slot(results, slot_id):
        start_row = starts[slot_id]
        row_count = counts[slot_id]
        weight_in = w_in[slot_id]
        weight_out = w_out[slot_id]

        def going(loop_state):
            return loop_state[0] * block_rows < row_count

        def step(loop_state):
            turn_index, buffer_rows = loop_state
            begin_row = (start_row + turn_index * block_rows).astype(jnp.int32)
            piece_rows = lax.dynamic_slice_in_dim(ordered, begin_row, block_rows, 0)
            gate_up = jnp.dot(piece_rows, weight_in.T, preferred_element_type=jnp.float32)
            hidden = (jax.nn.silu(gate_up[:, :FF]) * gate_up[:, FF:]).astype(jnp.bfloat16)
            made_rows = jnp.dot(hidden, weight_out, preferred_element_type=jnp.float32).astype(jnp.bfloat16)
            keep_rows = (jnp.arange(block_rows, dtype=jnp.int32) + turn_index * block_rows) < row_count
            current = lax.dynamic_slice_in_dim(buffer_rows, begin_row, block_rows, 0)
            buffer_rows = lax.dynamic_update_slice_in_dim(buffer_rows, jnp.where(keep_rows[:, None], made_rows, current), begin_row, 0)
            return turn_index + 1, buffer_rows

        _, results = lax.while_loop(going, step, (jnp.array(0, jnp.int32), results))
        return results, None

    results = jnp.zeros((row_total + block_rows, feat_width), jnp.bfloat16)
    results, _ = lax.scan(per_slot, results, jnp.arange(SLOTS, dtype=jnp.int32))
    made_all = jnp.zeros((row_total, feat_width), jnp.bfloat16).at[sorted_idx].set(results[:row_total])
    combined = jnp.sum(made_all.astype(jnp.float32).reshape(-1, TOPK, feat_width) * route_weight[:, :, None], axis=1)
    return combined.astype(jnp.bfloat16)


def reference(tokens, route_weight, routes, replica, old_place, new_src, w_in, w_out, queries, latent_cache, block_req, block_len):
    slot_first = slot_of_route(old_place, routes[0], replica[0])
    new_expert = old_place[new_src]
    slot_second = slot_of_route(new_expert, routes[1], replica[1])
    batch_one = moe_reference(tokens[0], route_weight[0], slot_first, w_in, w_out)
    batch_two = moe_reference(tokens[1], route_weight[1], new_src[slot_second].astype(jnp.int32), w_in, w_out)
    moe_out = jnp.stack([batch_one, batch_two])
    group_queries = queries.reshape(2 * N_GROUP, REQ_GROUP, H, KDIM)
    group_cache = latent_cache.reshape(2 * N_GROUP, CH_GROUP, SPAN, KDIM)
    group_req = block_req.reshape(2 * N_GROUP, CH_GROUP)
    group_len = block_len.reshape(2 * N_GROUP, CH_GROUP)

    def one_group(inputs):
        req_max, req_total, req_out = block_attention(inputs[0], inputs[1], inputs[2], inputs[3], LAT)
        return (req_out / req_total[:, :, None]).astype(jnp.bfloat16)

    attention = lax.map(one_group, (group_queries, group_cache, group_req, group_len))
    return moe_out, attention.reshape(2, REQS, H, LAT)
```

```python
from functools import partial

import jax
import jax.numpy as jnp
from jax import lax
from jax.experimental import pallas as pl
from jax.experimental.pallas import tpu as pltpu
from jax.sharding import PartitionSpec as P

MESH = pl.DeviceIdType.MESH
FF = 1408
EXPERTS = 64
TOPK = 6
LAT = 512
MOST = 6
CHUNKS = 8
DEPTH = 4
LAG = 3


score_scale = 192.0 ** (-0.5)
floor_value = -1e30


def block_attention(queries, latent_cache, block_req, block_len, latent):
    requests, head_count, feat_width = queries.shape
    blocks, cache_rows, _ = latent_cache.shape
    belongs = block_req[:, None] == jnp.arange(requests, dtype=jnp.int32)[None, :]
    chosen = jnp.dot(
        belongs.astype(jnp.bfloat16),
        queries.reshape(requests, head_count * feat_width),
        preferred_element_type=jnp.float32,
    )
    chosen = chosen.astype(jnp.bfloat16).reshape(blocks, head_count, feat_width)
    scores = (
        jnp.einsum("chk,cpk->chp", chosen, latent_cache, preferred_element_type=jnp.float32)
        * score_scale
    )
    live_rows = jnp.arange(cache_rows, dtype=jnp.int32)[None, :] < block_len[:, None]
    scores = jnp.where(live_rows[:, None, :], scores, floor_value)
    block_max = jnp.max(scores, axis=2)
    req_max = jnp.max(jnp.where(belongs[:, :, None], block_max[:, None, :], floor_value), axis=0)
    own_max = jnp.sum(jnp.where(belongs[:, :, None], req_max[None, :, :], 0.0), axis=1)
    exp_scores = jnp.where(live_rows[:, None, :], jnp.exp(scores - own_max[:, :, None]), 0.0)
    block_total = jnp.sum(exp_scores, axis=2)
    weights = exp_scores.astype(jnp.bfloat16)
    block_out = jnp.einsum(
        "chp,cpl->chl", weights, latent_cache[:, :, :latent], preferred_element_type=jnp.float32
    )
    belongs_f = belongs.astype(jnp.float32)
    req_total = jnp.einsum("cr,ch->rh", belongs_f, block_total, precision=lax.Precision.HIGHEST)
    req_out = jnp.einsum("cr,chl->rhl", belongs_f, block_out, precision=lax.Precision.HIGHEST)
    return (req_max, req_total, req_out)


def split_attention(req_max, req_total, req_out, n):
    batches, requests, heads, latent = req_out.shape
    share = batches * requests * heads // n
    stats = jnp.stack([req_max.reshape(n, share), req_total.reshape(n, share)], axis=2)
    stats = jnp.pad(stats, ((0, 0), (0, 0), (0, 126)))
    return stats, req_out.astype(jnp.bfloat16).reshape(n, share, latent)


def replica_keys(expert_of_slot):
    slots = expert_of_slot.shape[0]
    index = jnp.arange(slots, dtype=jnp.int32)
    earlier = (expert_of_slot[None, :] == expert_of_slot[:, None]) & (index[None, :] < index[:, None])
    return expert_of_slot * 2 + jnp.sum(earlier.astype(jnp.int32), axis=1)


def table_lookup(indices, lookup_table):
    matches = indices[:, None] == jnp.arange(lookup_table.shape[0], dtype=jnp.int32)[None, :]
    return jnp.sum(jnp.where(matches, lookup_table[None, :], 0), axis=1)


def greet(partners):
    barrier = pltpu.get_barrier_semaphore()
    for device in partners:
        pl.semaphore_signal(barrier, inc=1, device_id=device, device_id_type=MESH)
    pl.semaphore_wait(barrier, len(partners))


def remote(src, dst, send, recv, device):
    return pltpu.make_async_remote_copy(
        src_ref=src, dst_ref=dst, send_sem=send, recv_sem=recv, device_id=device, device_id_type=MESH
    )


def layer_kernel(
    length, n_inner, tok, meta, stats, parts, w_in, w_out, out, whole,
    zg, box, got, back, metas, tab, wei, ownf, ra, rz, acc, win, wout, got_stats, got_parts, joined,
    ms, mr, zs, zr, gs, gr, rs, rr, bs, br, xs, xr, ys, yr, ss, sr, qs, qr, js, jr, jl, wi, wo,
):
    L, Z = length, DEPTH
    n_dst = 2 * L
    slot_dev, ff = w_in.shape[0], w_in.shape[2]
    pieces = ff // wout.shape[1]
    part_ff = ff // pieces
    steps = pieces * slot_dev
    tokens = tok.shape[1]
    w = tok.shape[2] // CHUNKS
    per_slot = box.shape[4]
    rows = n_dst * slot_dev * per_slot
    count = L * Z * tokens

    g, i = lax.axis_index("group"), lax.axis_index("inner")
    x, core = g // 2, lax.rem(g, 2)
    z, y = i // L, lax.rem(i, L)
    a = x * (1 - core) + y * core
    r = y * (1 - core) + x * core

    def place(px, py, pz, pc):
        return (px * 2 + pc, pz * L + py)

    def dev(pa, pr, pz, pc):
        return place(pa * (1 - core) + pr * core, pr * (1 - core) + pa * core, pz, pc)

    mine = a * Z + z
    dst_self = r * 2 + core
    src_self = core * L + r
    mates = [lax.rem(mine + k, L * Z) for k in range(1, L * Z)]
    mates = [dev(m // Z, r, lax.rem(m, Z), core) for m in mates]
    inner_to = [lax.rem(i + k, n_inner) for k in range(1, n_inner)]
    routes_to = [lax.rem(r + k, L) for k in range(1, L)]
    gather_to = [lax.rem(a + k, L) for k in range(1, L)]
    other = 1 - core

    def fetch(step):
        s, h, buf = step // pieces, lax.rem(step, pieces), lax.rem(step, 2)
        at = pl.ds(pl.multiple_of(h * part_ff, 32), part_ff)
        return [
            pltpu.make_async_copy(w_in.at[s, :, at, :], win.at[buf], wi.at[buf]),
            pltpu.make_async_copy(w_out.at[s, at, :], wout.at[buf], wo.at[buf]),
        ]

    for copy in fetch(0):
        copy.start()

    greet(
        mates
        + [dev(a, p, z, core) for p in routes_to]
        + [dev(a, p, z, other) for p in routes_to]
        + [dev(p, r, z, other) for p in gather_to]
        + [dev(a, r, z, other)]
        + [(g, p) for p in inner_to]
    )

    def cols(c):
        return pl.ds(pl.multiple_of(c * w, w), w)

    def zcopy(b, c, k):
        return remote(
            tok.at[b, :, cols(c)], zg.at[b, c, a, z], zs.at[b, c, k - 1], zr.at[b, c, k - 1],
            dev(a, r, lax.rem(z + k, Z), core),
        )

    def gcopy(b, c, k):
        return remote(
            zg.at[b, c, a], zg.at[b, c, a], gs.at[b, c, k - 1], gr.at[b, c, k - 1],
            dev(lax.rem(a + k, L), r, z, core),
        )

    def rcopy(b, c, k):
        j = lax.rem(dst_self + k, n_dst)
        return remote(
            box.at[b, c, j], got.at[b, c, core, r], rs.at[b, c, k - 1], rr.at[b, c, k - 1],
            dev(a, j // 2, z, lax.rem(j, 2)),
        )

    def bcopy(b, s, k):
        idx = lax.rem(src_self + k, n_dst)
        pc, p = idx // L, lax.rem(idx, L)
        j = (y * (1 - pc) + x * pc) * 2 + core
        return remote(
            box.at[b, :, idx, s], back.at[b, :, j, s], bs.at[b, s, k - 1], br.at[b, s, j],
            place(x * (1 - pc) + p * pc, p * (1 - pc) + y * pc, z, pc),
        )

    def bwait(b, s, k):
        j = lax.rem(dst_self + k, n_dst)
        remote(
            box.at[b, :, j, s], back.at[b, :, j, s], bs.at[b, s, k - 1], br.at[b, s, j],
            dev(a, j // 2, z, lax.rem(j, 2)),
        ).wait_recv()

    def xcopy(b, c, k):
        p = lax.rem(a + k, L)
        return remote(
            zg.at[b, c, p], ra.at[b, c, k - 1], xs.at[b, c, k - 1], xr.at[b, c, k - 1], dev(p, r, z, core)
        )

    def ycopy(b, c, k):
        p = lax.rem(z + k, Z)
        return remote(
            zg.at[b, c, a, p], rz.at[b, c, k - 1], ys.at[b, c, k - 1], yr.at[b, c, k - 1], dev(a, r, p, core)
        )

    def z_send(b, c):
        for k in (1, 3, 2):
            zcopy(b, c, k).start()

    def g_send(b, c):
        for k in range(1, Z):
            zcopy(b, c, k).wait()
        for k in range(1, L):
            gcopy(b, c, k).start()

    def r_send(b, c):
        for k in range(1, L):
            gcopy(b, c, k).wait()
        made = jnp.dot(tab[b], zg[b, c].reshape(count, w), preferred_element_type=jnp.float32)
        box[b, c] = made.astype(jnp.bfloat16).reshape(box.shape[2:])
        for k in range(1, n_dst):
            rcopy(b, c, k).start()
        got[b, c, core, r] = box[b, c, dst_self]

    def r_wait(b):
        def one(c, carry):
            for k in range(1, n_dst):
                rcopy(b, c, k).wait()
            return carry

        lax.fori_loop(0, CHUNKS, one, 0)

    def expert(b, t):
        s, h, buf = t // pieces, lax.rem(t, pieces), lax.rem(t, 2)
        for copy in fetch(t):
            copy.wait()

        def ahead():
            for copy in fetch(lax.rem(t + 1, steps)):
                copy.start()

        if b == 0:
            ahead()
        else:
            pl.when(t < steps - 1)(ahead)
        contract = (((1,), (1,)), ((), ()))
        split = 1 if n_dst * per_slot <= 384 else 2
        group, part = 2 // split, n_dst * per_slot // split
        for q in range(split):
            at = slice(q * part, (q + 1) * part)
            arrived = jnp.concatenate(
                [got[b, c, q * group : (q + 1) * group, :, s].reshape(part, w) for c in range(CHUNKS)], axis=1
            )
            gate = lax.dot_general(arrived, win[buf, 0], contract, preferred_element_type=jnp.float32)
            up = lax.dot_general(arrived, win[buf, 1], contract, preferred_element_type=jnp.float32)
            hidden = (gate / (1.0 + jnp.exp(-gate)) * up).astype(jnp.bfloat16)
            made = jnp.dot(hidden, wout[buf], preferred_element_type=jnp.float32)

            @pl.when(h == 0)
            def _():
                acc[at, :] = made

            @pl.when((h > 0) & (h < pieces - 1))
            def _():
                acc[at, :] = acc[at, :] + made

            @pl.when(h == pieces - 1)
            def _():
                total = (acc[at, :] + made).astype(jnp.bfloat16)
                for c in range(CHUNKS):
                    box[b, c, q * group * L : (q + 1) * group * L, s] = total[:, c * w : (c + 1) * w].reshape(
                        group * L, per_slot, w
                    )

        @pl.when(h == pieces - 1)
        def _():
            for k in range(1, n_dst):
                bcopy(b, s, k).start()
            back[b, :, dst_self, s] = box[b, :, src_self, s]

    def b_wait(b):
        def one(s, carry):
            for k in range(1, n_dst):
                bwait(b, s, k)
            return carry

        lax.fori_loop(0, slot_dev, one, 0)

    def combine(b, c):
        made = jnp.dot(wei[b], back[b, c].reshape(rows, w), preferred_element_type=jnp.float32)
        made = made.reshape(L, Z, tokens, w)
        zg[b, c] = made.astype(jnp.bfloat16)
        for k in range(1, L):
            xcopy(b, c, k).start()
        for p in range(L):

            @pl.when(a == p)
            def _():
                ownf[c] = made[p]

    def z_stage(b, c):
        for k in range(1, L):
            xcopy(b, c, k).wait()
        total = ownf[c]
        for k in range(1, L):
            total = total + ra[b, c, k - 1].astype(jnp.float32)
        ownf[c] = total
        zg[b, c, a] = total.astype(jnp.bfloat16)
        for k in (1, 3, 2):
            ycopy(b, c, k).start()

    def finish(b, c):
        for k in range(1, Z):
            ycopy(b, c, k).wait()
        total = ownf[c, z]
        for k in range(1, Z):
            total = total + rz[b, c, k - 1].astype(jnp.float32)
        out[b, :, cols(c)] = total.astype(jnp.bfloat16)

    def give_back(b, n):
        pl.when(n < CHUNKS)(lambda: combine(b, n))
        pl.when((n >= 1) & (n < CHUNKS + 1))(lambda: z_stage(b, n - 1))
        pl.when(n >= 2)(lambda: finish(b, n - 2))

    told = [
        remote(meta, metas.at[mine], ms.at[k], mr.at[k], device) for k, device in enumerate(mates)
    ]
    for copy in told:
        copy.start()

    def first(c, carry):
        z_send(0, c)
        return carry

    lax.fori_loop(0, CHUNKS, first, 0)
    shares = []
    for k, p in enumerate(inner_to):
        shares.append(remote(stats.at[p], got_stats.at[i], ss.at[k], sr.at[k], (g, p)))
        shares.append(remote(parts.at[p], got_parts.at[i], qs.at[k], qr.at[k], (g, p)))
    for copy in shares:
        copy.start()

    def keep(c, carry):
        for b in range(2):
            zg[b, c, a, z] = tok[b, :, cols(c)]
        return carry

    lax.fori_loop(0, CHUNKS, keep, 0)
    metas[mine] = meta[...]
    got_stats[i] = stats[i]
    got_parts[i] = parts[i]
    for copy in told:
        copy.wait()
    step = 256
    pairs = L * Z // 2
    tiles = rows // step

    def fill(n, carry):
        t, p = n // pairs, lax.rem(n, pairs)
        lane = lax.broadcasted_iota(jnp.int32, (16, 2 * tokens), 1)
        index = lax.broadcasted_iota(jnp.int32, (step, 2 * tokens), 0) + t * step + mine * rows
        index = index.astype(jnp.float32)
        for b in range(2):
            both = jnp.where(lane < tokens, metas[2 * p, b], metas[2 * p + 1, b])
            chosen = jnp.zeros(index.shape, jnp.float32)
            weight = jnp.zeros(index.shape, jnp.float32)
            for k in range(TOPK):
                hit = index == both[k : k + 1, :]
                chosen = jnp.where(hit, 1.0, chosen)
                weight = jnp.where(hit, both[8 + k : 9 + k, :], weight)
            at = pl.ds(pl.multiple_of(t * step, step), step)
            span = pl.ds(pl.multiple_of(p * 2 * tokens, 128), 2 * tokens)
            tab[b, at, span] = chosen.astype(jnp.bfloat16)
            wei[b, span, at] = weight.T.astype(jnp.bfloat16)
        return carry

    lax.fori_loop(0, tiles * pairs, fill, 0)

    def send_first(c, carry):
        g_send(0, c)
        z_send(1, c)
        pl.when(c > 0)(lambda: r_send(0, c - 1))
        return carry

    lax.fori_loop(0, CHUNKS, send_first, 0)
    r_send(0, CHUNKS - 1)
    for copy in shares:
        copy.wait()
    joint = got_stats[0, :, 0:1]
    for p in range(1, n_inner):
        joint = jnp.maximum(joint, got_stats[p, :, 0:1])
    total = jnp.zeros_like(joint)
    summed = jnp.zeros(joined.shape, jnp.float32)
    for p in range(n_inner):
        scale = jnp.exp(got_stats[p, :, 0:1] - joint)
        total = total + got_stats[p, :, 1:2] * scale
        summed = summed + got_parts[p].astype(jnp.float32) * scale
    joined[...] = (summed / total).astype(jnp.bfloat16)
    spread = [remote(joined, whole.at[i], js.at[k], jr.at[k], (g, p)) for k, p in enumerate(inner_to)]
    spread.append(pltpu.make_async_copy(joined, whole.at[i], jl))
    for copy in spread:
        copy.start()
    g_send(1, 0)
    g_send(1, 1)
    r_wait(0)

    per_step = CHUNKS // steps

    def second(t, carry):
        for u in range(per_step):
            c = t * per_step + u + 2
            pl.when(c < CHUNKS)(lambda: g_send(1, c))
        expert(0, t)
        for u in range(per_step):
            r_send(1, t * per_step + u)
        return carry

    lax.fori_loop(0, steps, second, 0)
    r_wait(1)

    lag = min(LAG, steps - 1)

    def third(t, carry):
        expert(1, t)
        pl.when(t == lag)(lambda: b_wait(0))
        pl.when(t >= lag)(lambda: give_back(0, t - lag))
        return carry

    lax.fori_loop(0, steps, third, 0)

    def rest(n, carry):
        give_back(0, n)
        return carry

    lax.fori_loop(steps - lag, CHUNKS + 2, rest, 0)
    b_wait(1)

    def fourth(n, carry):
        give_back(1, n)
        return carry

    lax.fori_loop(0, CHUNKS + 2, fourth, 0)

    def drain(s, carry):
        for b in range(2):
            for k in range(1, n_dst):
                bcopy(b, s, k).wait_send()
        return carry

    lax.fori_loop(0, slot_dev, drain, 0)
    for copy in spread:
        copy.wait()


def layer(tokens, route_weight, slots, w_in, w_out, stats, parts):
    n_group, n_inner = lax.axis_size("group"), lax.axis_size("inner")
    batches, tok_count, width = tokens.shape
    slot_dev = w_in.shape[0]
    length = n_group // 2
    assert n_inner == length * DEPTH and 2 * tok_count == 128
    per_slot = length * DEPTH * MOST
    n_dst = 2 * length
    rows = n_dst * slot_dev * per_slot
    count = length * DEPTH * tok_count
    chunk = width // CHUNKS
    part_ff = FF // (2 if n_dst * per_slot <= 384 else 4)
    order = jnp.arange(tok_count * TOPK, dtype=jnp.int32)
    same = (slots[:, :, None] == slots[:, None, :]) & (order[None, None, :] < order[None, :, None])
    position = jnp.sum(same.astype(jnp.int32), axis=2)
    device, local_slot = slots // slot_dev, slots % slot_dev
    dev_group, dev_inner = device // n_inner, device % n_inner
    dev_x, dev_core, dev_z, dev_y = dev_group // 2, dev_group % 2, dev_inner // length, dev_inner % length
    g, i = lax.axis_index("group"), lax.axis_index("inner")
    along_x = g % 2 == 0
    dev_a, dev_r = jnp.where(along_x, dev_x, dev_y), jnp.where(along_x, dev_y, dev_x)
    mine = jnp.where(along_x, g // 2, i % length) * DEPTH + i // length
    row = (dev_a * DEPTH + dev_z) * rows
    row = row + ((dev_r * 2 + dev_core) * slot_dev + local_slot) * per_slot + mine * MOST + position
    row = row.reshape(batches, tok_count, TOPK).transpose(0, 2, 1).astype(jnp.float32)
    weight = route_weight.transpose(0, 2, 1)
    meta = jnp.concatenate(
        [
            jnp.pad(row, ((0, 0), (0, 2), (0, 0)), constant_values=-1.0),
            jnp.pad(weight, ((0, 0), (0, 2), (0, 0))),
        ],
        axis=1,
    )
    meta = jnp.concatenate([meta, meta], axis=2)
    vmem, hbm = pl.BlockSpec(memory_space=pltpu.VMEM), pl.BlockSpec(memory_space=pl.ANY)
    sem = pltpu.SemaphoreType.DMA
    bf16, f32 = jnp.bfloat16, jnp.float32
    boxes = pltpu.VMEM((2, CHUNKS, n_dst, slot_dev, per_slot, chunk), bf16)
    return pl.pallas_call(
        partial(layer_kernel, length, n_inner),
        out_shape=(
            jax.ShapeDtypeStruct(tokens.shape, bf16),
            jax.ShapeDtypeStruct(parts.shape, bf16),
        ),
        in_specs=[vmem] * 4 + [hbm] * 2,
        out_specs=(vmem, hbm),
        scratch_shapes=[
            pltpu.VMEM((2, CHUNKS, length, DEPTH, tok_count, chunk), bf16),
            boxes,
            pltpu.VMEM((2, CHUNKS, 2, length, slot_dev, per_slot, chunk), bf16),
            boxes,
            pltpu.VMEM((length * DEPTH,) + meta.shape, f32),
            pltpu.VMEM((2, rows, count), bf16),
            pltpu.VMEM((2, count, rows), bf16),
            pltpu.VMEM((CHUNKS, DEPTH, tok_count, chunk), f32),
            pltpu.VMEM((2, CHUNKS, length - 1, DEPTH, tok_count, chunk), bf16),
            pltpu.VMEM((2, CHUNKS, DEPTH - 1, tok_count, chunk), bf16),
            pltpu.VMEM((n_dst * per_slot, width), f32),
            pltpu.VMEM((2, 2, part_ff, width), bf16),
            pltpu.VMEM((2, part_ff, width), bf16),
            pltpu.VMEM(stats.shape, f32),
            pltpu.VMEM(parts.shape, bf16),
            pltpu.VMEM(parts.shape[1:], bf16),
        ]
        + [sem((length * DEPTH,))] * 2
        + [sem((2, CHUNKS, DEPTH - 1))] * 2
        + [sem((2, CHUNKS, length - 1))] * 2
        + [sem((2, CHUNKS, n_dst - 1))] * 2
        + [sem((2, slot_dev, n_dst))] * 2
        + [sem((2, CHUNKS, length - 1))] * 2
        + [sem((2, CHUNKS, DEPTH - 1))] * 2
        + [sem((n_inner,))] * 6
        + [sem]
        + [sem((2,))] * 2,
        compiler_params=pltpu.CompilerParams(
            collective_id=1, has_side_effects=True, vmem_limit_bytes=62 * 2**20
        ),
        cost_estimate=pl.CostEstimate(
            flops=6 * batches * slot_dev * n_dst * per_slot * FF * width,
            bytes_accessed=6 * batches * slot_dev * FF * width,
            transcendentals=0,
        ),
        name="layer",
    )(tokens, meta, stats, parts, w_in.reshape(slot_dev, 2, FF, width), w_out)


def local(
    tokens,
    route_weight,
    routes,
    replica,
    old_place,
    new_src,
    w_in,
    w_out,
    queries,
    latent_cache,
    block_req,
    block_len,
):
    slot_index = jnp.arange(old_place.shape[0], dtype=jnp.int32)
    keys = jnp.stack([replica_keys(old_place), replica_keys(table_lookup(new_src, old_place))])
    weight_slot = jnp.stack([slot_index, new_src])
    route_key = (routes * 2 + replica).reshape(2, -1)
    slots = jnp.sum(
        jnp.where(route_key[:, :, None] == keys[:, None, :], weight_slot[:, None, :], 0), axis=2
    )
    attend = jax.vmap(partial(block_attention, latent=LAT))
    partial_attention = attend(queries, latent_cache, block_req, block_len)
    stats, parts = split_attention(*partial_attention, lax.axis_size("inner"))
    moe_out, attention = layer(tokens, route_weight, slots, w_in, w_out, stats, parts)
    attention = attention.reshape(queries.shape[:3] + (LAT,))
    return (moe_out, attention)


def solution(mesh):
    in_specs = (
        P(None, ("group", "inner"), None),
        P(None, ("group", "inner"), None),
        P(None, ("group", "inner"), None),
        P(None, ("group", "inner"), None),
        P(),
        P(),
        P(("group", "inner"), None, None),
        P(("group", "inner"), None, None),
        P(None, "group", None, None),
        P(None, ("group", "inner"), None, None),
        P(None, ("group", "inner")),
        P(None, ("group", "inner")),
    )
    out_specs = (P(None, ("group", "inner"), None), P(None, "group", None, None))
    return jax.shard_map(local, mesh=mesh, in_specs=in_specs, out_specs=out_specs, check_vma=False)
```

```python
from functools import partial

import jax
import jax.numpy as jnp
from jax import lax
from jax.experimental import pallas as pl
from jax.experimental.pallas import tpu as pltpu
from jax.sharding import PartitionSpec as P

MESH = pl.DeviceIdType.MESH
FF = 1408
EXPERTS = 64
TOPK = 6
LAT = 512
MOST = 6
CHUNKS = 8
DEPTH = 4
HEADS = 16
LAG = 0
AFTER = 2
EARLY = 4


score_scale = 192.0 ** (-0.5)
floor_value = -1e30


def replica_keys(expert_of_slot):
    slots = expert_of_slot.shape[0]
    index = jnp.arange(slots, dtype=jnp.int32)
    earlier = (expert_of_slot[None, :] == expert_of_slot[:, None]) & (index[None, :] < index[:, None])
    return expert_of_slot * 2 + jnp.sum(earlier.astype(jnp.int32), axis=1)


def table_lookup(indices, lookup_table):
    matches = indices[:, None] == jnp.arange(lookup_table.shape[0], dtype=jnp.int32)[None, :]
    return jnp.sum(jnp.where(matches, lookup_table[None, :], 0), axis=1)


def greet(partners):
    barrier = pltpu.get_barrier_semaphore()
    for device in partners:
        pl.semaphore_signal(barrier, inc=1, device_id=device, device_id_type=MESH)
    pl.semaphore_wait(barrier, len(partners))


def remote(src, dst, send, recv, device):
    return pltpu.make_async_remote_copy(
        src_ref=src, dst_ref=dst, send_sem=send, recv_sem=recv, device_id=device, device_id_type=MESH
    )


def layer_kernel(
    length, n_inner, breq, blen, meta, ask, tok, cache, w_in, w_out, out, whole,
    zg, box, got, back, metas, tab, wei, ownf, ra, rz, acc, win, wout, got_stats, got_parts, joined,
    blocks, best, sums, mix, stats, parts, ks, cs, ms, mr, zs, zr, gs, gr, rs, rr, bs, br, xs, xr, ys, yr, ss, sr, qs, qr, js, jr, jl, wi, wo,
):
    L, Z = length, DEPTH
    n_dst = 2 * L
    slot_dev, ff = w_in.shape[0], w_in.shape[2]
    pieces = ff // wout.shape[1]
    part_ff = ff // pieces
    steps = pieces * slot_dev
    tokens = tok.shape[1]
    w = tok.shape[2] // CHUNKS
    per_slot = box.shape[4]
    rows = n_dst * slot_dev * per_slot
    count = L * Z * tokens

    g, i = lax.axis_index("group"), lax.axis_index("inner")
    x, core = g // 2, lax.rem(g, 2)
    z, y = i // L, lax.rem(i, L)
    a = x * (1 - core) + y * core
    r = y * (1 - core) + x * core

    def place(px, py, pz, pc):
        return (px * 2 + pc, pz * L + py)

    def dev(pa, pr, pz, pc):
        return place(pa * (1 - core) + pr * core, pr * (1 - core) + pa * core, pz, pc)

    mine = a * Z + z
    dst_self = r * 2 + core
    src_self = core * L + r
    mates = [lax.rem(mine + k, L * Z) for k in range(1, L * Z)]
    mates = [dev(m // Z, r, lax.rem(m, Z), core) for m in mates]
    inner_to = [lax.rem(i + k, n_inner) for k in range(1, n_inner)]
    routes_to = [lax.rem(r + k, L) for k in range(1, L)]
    gather_to = [lax.rem(a + k, L) for k in range(1, L)]
    other = 1 - core

    def fetch(step):
        s, h, buf = step // pieces, lax.rem(step, pieces), lax.rem(step, 2)
        at = pl.ds(pl.multiple_of(h * part_ff, 16), part_ff)
        return [
            pltpu.make_async_copy(w_in.at[s, :, at, :], win.at[buf], wi.at[buf]),
            pltpu.make_async_copy(w_out.at[s, at, :], wout.at[buf], wo.at[buf]),
        ]

    for copy in fetch(0):
        copy.start()

    greet(
        mates
        + [dev(a, p, z, core) for p in routes_to]
        + [dev(a, p, z, other) for p in routes_to]
        + [dev(p, r, z, other) for p in gather_to]
        + [dev(a, r, z, other)]
        + [(g, p) for p in inner_to]
    )

    def cols(c):
        return pl.ds(pl.multiple_of(c * w, w), w)

    def zcopy(b, c, k):
        return remote(
            tok.at[b, :, cols(c)], zg.at[b, c, a, z], zs.at[b, c, k - 1], zr.at[b, c, k - 1],
            dev(a, r, lax.rem(z + k, Z), core),
        )

    def gcopy(b, c, k):
        return remote(
            zg.at[b, c, a], zg.at[b, c, a], gs.at[b, c, k - 1], gr.at[b, c, k - 1],
            dev(lax.rem(a + k, L), r, z, core),
        )

    def rcopy(b, c, k):
        j = lax.rem(dst_self + k, n_dst)
        return remote(
            box.at[b, c, j], got.at[b, c, core, r], rs.at[b, c, k - 1], rr.at[b, c, k - 1],
            dev(a, j // 2, z, lax.rem(j, 2)),
        )

    def bcopy(b, s, k):
        idx = lax.rem(src_self + k, n_dst)
        pc, p = idx // L, lax.rem(idx, L)
        j = (y * (1 - pc) + x * pc) * 2 + core
        return remote(
            box.at[b, :, idx, s], back.at[b, :, j, s], bs.at[b, s, k - 1], br.at[b, s, j],
            place(x * (1 - pc) + p * pc, p * (1 - pc) + y * pc, z, pc),
        )

    def bwait(b, s, k):
        j = lax.rem(dst_self + k, n_dst)
        remote(
            box.at[b, :, j, s], back.at[b, :, j, s], bs.at[b, s, k - 1], br.at[b, s, j],
            dev(a, j // 2, z, lax.rem(j, 2)),
        ).wait_recv()

    def xcopy(b, c, k):
        p = lax.rem(a + k, L)
        return remote(
            zg.at[b, c, p], ra.at[b, c, k - 1], xs.at[b, c, k - 1], xr.at[b, c, k - 1], dev(p, r, z, core)
        )

    def ycopy(b, c, k):
        p = lax.rem(z + k, Z)
        return remote(
            zg.at[b, c, a, p], rz.at[b, c, k - 1], ys.at[b, c, k - 1], yr.at[b, c, k - 1], dev(a, r, p, core)
        )

    def z_send(b, c):
        for k in (1, 3, 2):
            zcopy(b, c, k).start()

    def kcopy(b, c):
        return pltpu.make_async_copy(tok.at[b, :, cols(c)], zg.at[b, c, a, z], ks.at[b, c])

    def g_send(b, c):
        kcopy(b, c).wait()
        for k in range(1, Z):
            zcopy(b, c, k).wait()
        for k in range(1, L):
            gcopy(b, c, k).start()

    def r_send(b, c):
        for k in range(1, L):
            gcopy(b, c, k).wait()
        made = jnp.dot(tab[b], zg[b, c].reshape(count, w), preferred_element_type=jnp.float32)
        box[b, c] = made.astype(jnp.bfloat16).reshape(box.shape[2:])
        for k in range(1, n_dst):
            rcopy(b, c, k).start()
        got[b, c, core, r] = box[b, c, dst_self]

    def r_wait(b):
        def one(c, carry):
            for k in range(1, n_dst):
                rcopy(b, c, k).wait()
            return carry

        lax.fori_loop(0, CHUNKS, one, 0)

    def expert(b, t):
        s, h, buf = t // pieces, lax.rem(t, pieces), lax.rem(t, 2)

        def ahead():
            for copy in fetch(lax.rem(t + 1, steps)):
                copy.start()

        if b == 0:
            ahead()
        else:
            pl.when(t < steps - 1)(ahead)
        for copy in fetch(t):
            copy.wait()
        contract = (((1,), (1,)), ((), ()))
        split = 1 if n_dst * per_slot <= 384 else 2
        group, part = 2 // split, n_dst * per_slot // split
        for q in range(split):
            at = slice(q * part, (q + 1) * part)
            arrived = jnp.concatenate(
                [got[b, c, q * group : (q + 1) * group, :, s].reshape(part, w) for c in range(CHUNKS)], axis=1
            )
            gate = lax.dot_general(arrived, win[buf, 0], contract, preferred_element_type=jnp.float32)
            up = lax.dot_general(arrived, win[buf, 1], contract, preferred_element_type=jnp.float32)
            hidden = (gate / (1.0 + jnp.exp(-gate)) * up).astype(jnp.bfloat16)
            made = jnp.dot(hidden, wout[buf], preferred_element_type=jnp.float32)

            @pl.when(h == 0)
            def _():
                acc[at, :] = made

            @pl.when((h > 0) & (h < pieces - 1))
            def _():
                acc[at, :] = acc[at, :] + made

            @pl.when(h == pieces - 1)
            def _():
                total = (acc[at, :] + made).astype(jnp.bfloat16)
                for c in range(CHUNKS):
                    box[b, c, q * group * L : (q + 1) * group * L, s] = total[:, c * w : (c + 1) * w].reshape(
                        group * L, per_slot, w
                    )

        @pl.when(h == pieces - 1)
        def _():
            for k in range(1, n_dst):
                bcopy(b, s, k).start()
            back[b, :, dst_self, s] = box[b, :, src_self, s]

    def b_wait(b):
        def one(s, carry):
            for k in range(1, n_dst):
                bwait(b, s, k)
            return carry

        lax.fori_loop(0, slot_dev, one, 0)

    def combine(b, c):
        made = jnp.dot(wei[b], back[b, c].reshape(rows, w), preferred_element_type=jnp.float32)
        made = made.reshape(L, Z, tokens, w)
        zg[b, c] = made.astype(jnp.bfloat16)
        for k in range(1, L):
            xcopy(b, c, k).start()
        for p in range(L):

            @pl.when(a == p)
            def _():
                ownf[c] = made[p]

    def z_stage(b, c):
        for k in range(1, L):
            xcopy(b, c, k).wait()
        total = ownf[c]
        for k in range(1, L):
            total = total + ra[b, c, k - 1].astype(jnp.float32)
        ownf[c] = total
        zg[b, c, a] = total.astype(jnp.bfloat16)
        for k in (1, 3, 2):
            ycopy(b, c, k).start()

    def finish(b, c):
        for k in range(1, Z):
            ycopy(b, c, k).wait()
        total = ownf[c, z]
        for k in range(1, Z):
            total = total + rz[b, c, k - 1].astype(jnp.float32)
        out[b, :, cols(c)] = total.astype(jnp.bfloat16)

    def give_back(b, n, one, two):
        pl.when(n < CHUNKS)(lambda: combine(b, n))
        pl.when((n >= one) & (n < CHUNKS + one))(lambda: z_stage(b, n - one))
        pl.when(n >= two)(lambda: finish(b, n - two))

    told = [
        remote(meta, metas.at[mine], ms.at[k], mr.at[k], device) for k, device in enumerate(mates)
    ]
    for copy in told:
        copy.start()

    def first(c, carry):
        z_send(0, c)
        return carry

    lax.fori_loop(0, CHUNKS, first, 0)

    def keep(c, carry):
        for b in range(2):
            kcopy(b, c).start()
        return carry

    lax.fori_loop(0, CHUNKS, keep, 0)

    batch_blocks = cache.shape[1]
    n_blocks = 2 * batch_blocks
    ring = blocks.shape[0]
    latent = mix.shape[2]

    def block_copy(n):
        slot = lax.rem(n, ring)
        return pltpu.make_async_copy(
            cache.at[n // batch_blocks, lax.rem(n, batch_blocks)], blocks.at[slot], cs.at[slot]
        )

    best[...] = jnp.full(best.shape, floor_value, jnp.float32)
    sums[...] = jnp.zeros_like(sums)
    mix[...] = jnp.zeros_like(mix)
    for n in range(ring - 1):
        block_copy(n).start()

    def attend(n):
        b, c = n // batch_blocks, lax.rem(n, batch_blocks)
        pl.when(n + ring - 1 < n_blocks)(lambda: block_copy(n + ring - 1).start())
        block_copy(n).wait()
        block = blocks[lax.rem(n, ring)]
        scores = lax.dot_general(
            ask[b], block, (((1,), (1,)), ((), ())), preferred_element_type=jnp.float32
        )
        scores = scores * score_scale
        head = lax.broadcasted_iota(jnp.int32, scores.shape, 0) // HEADS
        key = lax.broadcasted_iota(jnp.int32, scores.shape, 1)
        live = (head == breq[b, c]) & (key < blen[b, c])
        scores = jnp.where(live, scores, floor_value)
        before = best[b]
        now = jnp.maximum(before, jnp.max(scores, axis=1, keepdims=True))
        fade = jnp.exp(before - now)
        weights = jnp.where(live, jnp.exp(scores - now[:, 0:1]), 0.0)
        best[b] = now
        sums[b] = sums[b] * fade + jnp.sum(weights, axis=1, keepdims=True)
        mix[b] = mix[b] * fade[:, 0:1] + jnp.dot(
            weights.astype(jnp.bfloat16), block[:, :latent], preferred_element_type=jnp.float32
        )

    metas[mine] = meta[...]
    for copy in told:
        copy.wait()
    step = 256
    pairs = L * Z // 2
    tiles = rows // step

    def fill(n, carry):
        t, p = n // pairs, lax.rem(n, pairs)
        lane = lax.broadcasted_iota(jnp.int32, (16, 2 * tokens), 1)
        index = lax.broadcasted_iota(jnp.int32, (step, 2 * tokens), 0) + t * step + mine * rows
        index = index.astype(jnp.float32)
        for b in range(2):
            both = jnp.where(lane < tokens, metas[2 * p, b], metas[2 * p + 1, b])
            chosen = jnp.zeros(index.shape, jnp.float32)
            weight = jnp.zeros(index.shape, jnp.float32)
            for k in range(TOPK):
                hit = index == both[k : k + 1, :]
                chosen = jnp.where(hit, 1.0, chosen)
                weight = jnp.where(hit, both[8 + k : 9 + k, :], weight)
            at = pl.ds(pl.multiple_of(t * step, step), step)
            span = pl.ds(pl.multiple_of(p * 2 * tokens, 128), 2 * tokens)
            tab[b, at, span] = chosen.astype(jnp.bfloat16)
            wei[b, span, at] = weight.T.astype(jnp.bfloat16)
        return carry

    lax.fori_loop(0, tiles * pairs, fill, 0)

    per_chunk = -(-n_blocks // CHUNKS)

    def send_first(c, carry):
        g_send(0, c)

        @pl.when(c >= CHUNKS // 2)
        def _():
            z_send(1, 2 * c - CHUNKS)
            z_send(1, 2 * c - CHUNKS + 1)

        for u in range(per_chunk):
            n = c * per_chunk + u
            pl.when(n < n_blocks)(lambda: attend(n))
        pl.when(c > 0)(lambda: r_send(0, c - 1))
        return carry

    lax.fori_loop(0, CHUNKS, send_first, 0)
    r_send(0, CHUNKS - 1)
    lane = lax.broadcasted_iota(jnp.int32, best.shape, 2)
    stats[...] = jnp.where(lane == 0, best[...], sums[...]).reshape(stats.shape)
    parts[...] = mix[...].reshape(parts.shape).astype(jnp.bfloat16)
    shares = []
    for k, p in enumerate(inner_to):
        shares.append(remote(stats.at[p], got_stats.at[i], ss.at[k], sr.at[k], (g, p)))
        shares.append(remote(parts.at[p], got_parts.at[i], qs.at[k], qr.at[k], (g, p)))
    for copy in shares:
        copy.start()
    got_stats[i] = stats[i]
    got_parts[i] = parts[i]

    def gather_second(c, carry):
        g_send(1, c)
        return carry

    lax.fori_loop(0, CHUNKS, gather_second, 0)

    def early_second(c, carry):
        r_send(1, c)
        return carry

    lax.fori_loop(0, EARLY, early_second, 0)
    r_wait(0)

    def second(t, carry):
        pl.when(t + EARLY < CHUNKS)(lambda: r_send(1, t + EARLY))
        expert(0, t)
        return carry

    assert steps + EARLY >= CHUNKS
    lax.fori_loop(0, steps, second, 0)
    for copy in shares:
        copy.wait()
    joint = got_stats[0, :, 0:1]
    for p in range(1, n_inner):
        joint = jnp.maximum(joint, got_stats[p, :, 0:1])
    total = jnp.zeros_like(joint)
    summed = jnp.zeros(joined.shape, jnp.float32)
    for p in range(n_inner):
        scale = jnp.exp(got_stats[p, :, 0:1] - joint)
        total = total + got_stats[p, :, 1:2] * scale
        summed = summed + got_parts[p].astype(jnp.float32) * scale
    joined[...] = (summed / total).astype(jnp.bfloat16)
    spread = [remote(joined, whole.at[i], js.at[k], jr.at[k], (g, p)) for k, p in enumerate(inner_to)]
    spread.append(pltpu.make_async_copy(joined, whole.at[i], jl))
    for copy in spread:
        copy.start()
    r_wait(1)

    lag = min(LAG, steps - 1)

    def third(t, carry):
        expert(1, t)
        pl.when(t == lag)(lambda: b_wait(0))
        pl.when(t >= lag)(lambda: give_back(0, t - lag, 1, 2))
        return carry

    lax.fori_loop(0, steps, third, 0)

    def rest(n, carry):
        give_back(0, n, 1, 2)
        return carry

    lax.fori_loop(steps - lag, CHUNKS + 2, rest, 0)
    b_wait(1)

    def fourth(n, carry):
        give_back(1, n, AFTER, 2 * AFTER + 1)
        return carry

    lax.fori_loop(0, CHUNKS + 2 * AFTER + 1, fourth, 0)

    def drain(s, carry):
        for b in range(2):
            for k in range(1, n_dst):
                bcopy(b, s, k).wait_send()
        return carry

    lax.fori_loop(0, slot_dev, drain, 0)
    for copy in spread:
        copy.wait()


def layer(tokens, route_weight, slots, w_in, w_out, queries, latent_cache, block_req, block_len):
    n_group, n_inner = lax.axis_size("group"), lax.axis_size("inner")
    batches, tok_count, width = tokens.shape
    requests, heads, feat_width = queries.shape[1:]
    asked = requests * heads
    share = batches * asked // n_inner
    assert heads == HEADS
    slot_dev = w_in.shape[0]
    length = n_group // 2
    assert n_inner == length * DEPTH and 2 * tok_count == 128
    per_slot = length * DEPTH * MOST
    n_dst = 2 * length
    rows = n_dst * slot_dev * per_slot
    count = length * DEPTH * tok_count
    chunk = width // CHUNKS
    part_ff = FF // (2 if n_dst * per_slot <= 384 else 8)
    order = jnp.arange(tok_count * TOPK, dtype=jnp.int32)
    same = (slots[:, :, None] == slots[:, None, :]) & (order[None, None, :] < order[None, :, None])
    position = jnp.sum(same.astype(jnp.int32), axis=2)
    device, local_slot = slots // slot_dev, slots % slot_dev
    dev_group, dev_inner = device // n_inner, device % n_inner
    dev_x, dev_core, dev_z, dev_y = dev_group // 2, dev_group % 2, dev_inner // length, dev_inner % length
    g, i = lax.axis_index("group"), lax.axis_index("inner")
    along_x = g % 2 == 0
    dev_a, dev_r = jnp.where(along_x, dev_x, dev_y), jnp.where(along_x, dev_y, dev_x)
    mine = jnp.where(along_x, g // 2, i % length) * DEPTH + i // length
    row = (dev_a * DEPTH + dev_z) * rows
    row = row + ((dev_r * 2 + dev_core) * slot_dev + local_slot) * per_slot + mine * MOST + position
    row = row.reshape(batches, tok_count, TOPK).transpose(0, 2, 1).astype(jnp.float32)
    weight = route_weight.transpose(0, 2, 1)
    meta = jnp.concatenate(
        [
            jnp.pad(row, ((0, 0), (0, 2), (0, 0)), constant_values=-1.0),
            jnp.pad(weight, ((0, 0), (0, 2), (0, 0))),
        ],
        axis=1,
    )
    meta = jnp.concatenate([meta, meta], axis=2)
    vmem, hbm = pl.BlockSpec(memory_space=pltpu.VMEM), pl.BlockSpec(memory_space=pl.ANY)
    sem = pltpu.SemaphoreType.DMA
    bf16, f32 = jnp.bfloat16, jnp.float32
    boxes = pltpu.VMEM((2, CHUNKS, n_dst, slot_dev, per_slot, chunk), bf16)
    return pl.pallas_call(
        partial(layer_kernel, length, n_inner),
        out_shape=(
            jax.ShapeDtypeStruct(tokens.shape, bf16),
            jax.ShapeDtypeStruct((n_inner, share, LAT), bf16),
        ),
        in_specs=[pl.BlockSpec(memory_space=pltpu.SMEM)] * 2 + [vmem] * 2 + [hbm] * 4,
        out_specs=(vmem, hbm),
        scratch_shapes=[
            pltpu.VMEM((2, CHUNKS, length, DEPTH, tok_count, chunk), bf16),
            boxes,
            pltpu.VMEM((2, CHUNKS, 2, length, slot_dev, per_slot, chunk), bf16),
            boxes,
            pltpu.VMEM((length * DEPTH,) + meta.shape, f32),
            pltpu.VMEM((2, rows, count), bf16),
            pltpu.VMEM((2, count, rows), bf16),
            pltpu.VMEM((CHUNKS, DEPTH, tok_count, chunk), f32),
            pltpu.VMEM((2, CHUNKS, length - 1, DEPTH, tok_count, chunk), bf16),
            pltpu.VMEM((2, CHUNKS, DEPTH - 1, tok_count, chunk), bf16),
            pltpu.VMEM((n_dst * per_slot, width), f32),
            pltpu.VMEM((2, 2, part_ff, width), bf16),
            pltpu.VMEM((2, part_ff, width), bf16),
            pltpu.VMEM((n_inner, share, 128), f32),
            pltpu.VMEM((n_inner, share, LAT), bf16),
            pltpu.VMEM((share, LAT), bf16),
            pltpu.VMEM((4,) + latent_cache.shape[2:], bf16),
            pltpu.VMEM((batches, asked, 128), f32),
            pltpu.VMEM((batches, asked, 128), f32),
            pltpu.VMEM((batches, asked, LAT), f32),
            pltpu.VMEM((n_inner, share, 128), f32),
            pltpu.VMEM((n_inner, share, LAT), bf16),
            sem((2, CHUNKS)),
            sem((4,)),
        ]
        + [sem((length * DEPTH,))] * 2
        + [sem((2, CHUNKS, DEPTH - 1))] * 2
        + [sem((2, CHUNKS, length - 1))] * 2
        + [sem((2, CHUNKS, n_dst - 1))] * 2
        + [sem((2, slot_dev, n_dst))] * 2
        + [sem((2, CHUNKS, length - 1))] * 2
        + [sem((2, CHUNKS, DEPTH - 1))] * 2
        + [sem((n_inner,))] * 6
        + [sem]
        + [sem((2,))] * 2,
        compiler_params=pltpu.CompilerParams(
            collective_id=1, has_side_effects=True, vmem_limit_bytes=62 * 2**20
        ),
        cost_estimate=pl.CostEstimate(
            flops=6 * batches * slot_dev * n_dst * per_slot * FF * width,
            bytes_accessed=6 * batches * slot_dev * FF * width,
            transcendentals=0,
        ),
        name="layer",
    )(
        block_req,
        block_len,
        meta,
        queries.reshape(batches, asked, feat_width),
        tokens,
        latent_cache,
        w_in.reshape(slot_dev, 2, FF, width),
        w_out,
    )


def local(
    tokens,
    route_weight,
    routes,
    replica,
    old_place,
    new_src,
    w_in,
    w_out,
    queries,
    latent_cache,
    block_req,
    block_len,
):
    slot_index = jnp.arange(old_place.shape[0], dtype=jnp.int32)
    keys = jnp.stack([replica_keys(old_place), replica_keys(table_lookup(new_src, old_place))])
    weight_slot = jnp.stack([slot_index, new_src])
    route_key = (routes * 2 + replica).reshape(2, -1)
    slots = jnp.sum(
        jnp.where(route_key[:, :, None] == keys[:, None, :], weight_slot[:, None, :], 0), axis=2
    )
    moe_out, attention = layer(
        tokens, route_weight, slots, w_in, w_out, queries, latent_cache, block_req, block_len
    )
    attention = attention.reshape(queries.shape[:3] + (LAT,))
    return (moe_out, attention)


def solution(mesh):
    in_specs = (
        P(None, ("group", "inner"), None),
        P(None, ("group", "inner"), None),
        P(None, ("group", "inner"), None),
        P(None, ("group", "inner"), None),
        P(),
        P(),
        P(("group", "inner"), None, None),
        P(("group", "inner"), None, None),
        P(None, "group", None, None),
        P(None, ("group", "inner"), None, None),
        P(None, ("group", "inner")),
        P(None, ("group", "inner")),
    )
    out_specs = (P(None, ("group", "inner"), None), P(None, "group", None, None))
    return jax.shard_map(local, mesh=mesh, in_specs=in_specs, out_specs=out_specs, check_vma=False)
```

```python
from functools import partial

import jax
import jax.numpy as jnp
from jax import lax
from jax.experimental import pallas as pl
from jax.experimental.pallas import tpu as pltpu
from jax.sharding import PartitionSpec as P

MESH = pl.DeviceIdType.MESH
FF = 1408
EXPERTS = 64
TOPK = 6
LAT = 512
MOST = 6
CHUNKS = 8
DEPTH = 4
HEADS = 16
HEAD = 2
AFTER = 2
EARLY = 4


score_scale = 192.0 ** (-0.5)
floor_value = -1e30


def replica_keys(expert_of_slot):
    slots = expert_of_slot.shape[0]
    index = jnp.arange(slots, dtype=jnp.int32)
    earlier = (expert_of_slot[None, :] == expert_of_slot[:, None]) & (index[None, :] < index[:, None])
    return expert_of_slot * 2 + jnp.sum(earlier.astype(jnp.int32), axis=1)


def table_lookup(indices, lookup_table):
    matches = indices[:, None] == jnp.arange(lookup_table.shape[0], dtype=jnp.int32)[None, :]
    return jnp.sum(jnp.where(matches, lookup_table[None, :], 0), axis=1)


def greet(partners):
    barrier = pltpu.get_barrier_semaphore()
    for device in partners:
        pl.semaphore_signal(barrier, inc=1, device_id=device, device_id_type=MESH)
    pl.semaphore_wait(barrier, len(partners))


def remote(src, dst, send, recv, device):
    return pltpu.make_async_remote_copy(
        src_ref=src, dst_ref=dst, send_sem=send, recv_sem=recv, device_id=device, device_id_type=MESH
    )


def layer_kernel(
    length, n_inner, breq, blen, meta, ask, tok, cache, w_in, w_out, out, whole,
    zg, box, got, back, metas, tab, wei, ownf, ra, rz, acc, win, wout, got_stats, got_parts, joined,
    blocks, best, sums, mix, stats, parts, ks, cs, ms, mr, zs, zr, gs, gr, rs, rr, bs, br, xs, xr, ys, yr, ss, sr, qs, qr, js, jr, jl, wi, wo,
):
    L, Z = length, DEPTH
    n_dst = 2 * L
    slot_dev, ff = w_in.shape[0], w_in.shape[2]
    pieces = ff // wout.shape[1]
    part_ff = ff // pieces
    steps = pieces * slot_dev
    tokens = tok.shape[1]
    w = tok.shape[2] // CHUNKS
    per_slot = box.shape[4]
    rows = n_dst * slot_dev * per_slot
    count = L * Z * tokens

    g, i = lax.axis_index("group"), lax.axis_index("inner")
    x, core = g // 2, lax.rem(g, 2)
    z, y = i // L, lax.rem(i, L)
    a = x * (1 - core) + y * core
    r = y * (1 - core) + x * core

    def place(px, py, pz, pc):
        return (px * 2 + pc, pz * L + py)

    def dev(pa, pr, pz, pc):
        return place(pa * (1 - core) + pr * core, pr * (1 - core) + pa * core, pz, pc)

    mine = a * Z + z
    dst_self = r * 2 + core
    src_self = core * L + r
    mates = [lax.rem(mine + k, L * Z) for k in range(1, L * Z)]
    mates = [dev(m // Z, r, lax.rem(m, Z), core) for m in mates]
    inner_to = [lax.rem(i + k, n_inner) for k in range(1, n_inner)]
    routes_to = [lax.rem(r + k, L) for k in range(1, L)]
    gather_to = [lax.rem(a + k, L) for k in range(1, L)]
    other = 1 - core

    def fetch(step):
        s, h, buf = step // pieces, lax.rem(step, pieces), lax.rem(step, 2)
        at = pl.ds(pl.multiple_of(h * part_ff, 16), part_ff)
        return [
            pltpu.make_async_copy(w_in.at[s, :, at, :], win.at[buf], wi.at[buf]),
            pltpu.make_async_copy(w_out.at[s, at, :], wout.at[buf], wo.at[buf]),
        ]

    for copy in fetch(0):
        copy.start()

    greet(
        mates
        + [dev(a, p, z, core) for p in routes_to]
        + [dev(a, p, z, other) for p in routes_to]
        + [dev(p, r, z, other) for p in gather_to]
        + [dev(a, r, z, other)]
        + [(g, p) for p in inner_to]
    )

    def cols(c):
        return pl.ds(pl.multiple_of(c * w, w), w)

    def zcopy(b, c, k):
        return remote(
            tok.at[b, :, cols(c)], zg.at[b, c, a, z], zs.at[b, c, k - 1], zr.at[b, c, k - 1],
            dev(a, r, lax.rem(z + k, Z), core),
        )

    def gcopy(b, c, k):
        return remote(
            zg.at[b, c, a], zg.at[b, c, a], gs.at[b, c, k - 1], gr.at[b, c, k - 1],
            dev(lax.rem(a + k, L), r, z, core),
        )

    def rcopy(b, c, k):
        j = lax.rem(dst_self + k, n_dst)
        return remote(
            box.at[b, c, j], got.at[b, c, core, r], rs.at[b, c, k - 1], rr.at[b, c, k - 1],
            dev(a, j // 2, z, lax.rem(j, 2)),
        )

    def bcopy(b, s, k):
        idx = lax.rem(src_self + k, n_dst)
        pc, p = idx // L, lax.rem(idx, L)
        j = (y * (1 - pc) + x * pc) * 2 + core
        return remote(
            box.at[b, :, idx, s], back.at[b, :, j, s], bs.at[b, s, k - 1], br.at[b, s, j],
            place(x * (1 - pc) + p * pc, p * (1 - pc) + y * pc, z, pc),
        )

    def bwait(b, s, k):
        j = lax.rem(dst_self + k, n_dst)
        remote(
            box.at[b, :, j, s], back.at[b, :, j, s], bs.at[b, s, k - 1], br.at[b, s, j],
            dev(a, j // 2, z, lax.rem(j, 2)),
        ).wait_recv()

    def xcopy(b, c, k):
        p = lax.rem(a + k, L)
        return remote(
            zg.at[b, c, p], ra.at[b, c, k - 1], xs.at[b, c, k - 1], xr.at[b, c, k - 1], dev(p, r, z, core)
        )

    def ycopy(b, c, k):
        p = lax.rem(z + k, Z)
        return remote(
            zg.at[b, c, a, p], rz.at[b, c, k - 1], ys.at[b, c, k - 1], yr.at[b, c, k - 1], dev(a, r, p, core)
        )

    def z_send(b, c):
        for k in (1, 3, 2):
            zcopy(b, c, k).start()

    def kcopy(b, c):
        return pltpu.make_async_copy(tok.at[b, :, cols(c)], zg.at[b, c, a, z], ks.at[b, c])

    def g_send(b, c):
        kcopy(b, c).wait()
        for k in range(1, Z):
            zcopy(b, c, k).wait()
        for k in range(1, L):
            gcopy(b, c, k).start()

    def r_send(b, c):
        for k in range(1, L):
            gcopy(b, c, k).wait()
        made = jnp.dot(tab[b], zg[b, c].reshape(count, w), preferred_element_type=jnp.float32)
        box[b, c] = made.astype(jnp.bfloat16).reshape(box.shape[2:])
        for k in range(1, n_dst):
            rcopy(b, c, k).start()
        got[b, c, core, r] = box[b, c, dst_self]

    def r_wait(b):
        def one(c, carry):
            for k in range(1, n_dst):
                rcopy(b, c, k).wait()
            return carry

        lax.fori_loop(0, CHUNKS, one, 0)

    def expert(b, t):
        s, h, buf = t // pieces, lax.rem(t, pieces), lax.rem(t, 2)

        def ahead():
            for copy in fetch(lax.rem(t + 1, steps)):
                copy.start()

        if b == 0:
            ahead()
        else:
            pl.when(t < steps - 1)(ahead)
        for copy in fetch(t):
            copy.wait()
        contract = (((1,), (1,)), ((), ()))
        split = 1 if n_dst * per_slot <= 384 else 2
        group, part = 2 // split, n_dst * per_slot // split
        for q in range(split):
            at = slice(q * part, (q + 1) * part)
            arrived = jnp.concatenate(
                [got[b, c, q * group : (q + 1) * group, :, s].reshape(part, w) for c in range(CHUNKS)], axis=1
            )
            gate = lax.dot_general(arrived, win[buf, 0], contract, preferred_element_type=jnp.float32)
            up = lax.dot_general(arrived, win[buf, 1], contract, preferred_element_type=jnp.float32)
            hidden = (gate / (1.0 + jnp.exp(-gate)) * up).astype(jnp.bfloat16)
            made = jnp.dot(hidden, wout[buf], preferred_element_type=jnp.float32)

            @pl.when(h == 0)
            def _():
                acc[at, :] = made

            @pl.when((h > 0) & (h < pieces - 1))
            def _():
                acc[at, :] = acc[at, :] + made

            @pl.when(h == pieces - 1)
            def _():
                total = (acc[at, :] + made).astype(jnp.bfloat16)
                for c in range(CHUNKS):
                    box[b, c, q * group * L : (q + 1) * group * L, s] = total[:, c * w : (c + 1) * w].reshape(
                        group * L, per_slot, w
                    )

        @pl.when(h == pieces - 1)
        def _():
            for k in range(1, n_dst):
                bcopy(b, s, k).start()
            back[b, :, dst_self, s] = box[b, :, src_self, s]

    def b_wait(b):
        def one(s, carry):
            for k in range(1, n_dst):
                bwait(b, s, k)
            return carry

        lax.fori_loop(0, slot_dev, one, 0)

    def combine(b, c):
        made = jnp.dot(wei[b], back[b, c].reshape(rows, w), preferred_element_type=jnp.float32)
        made = made.reshape(L, Z, tokens, w)
        zg[b, c] = made.astype(jnp.bfloat16)
        for k in range(1, L):
            xcopy(b, c, k).start()
        for p in range(L):

            @pl.when(a == p)
            def _():
                ownf[c] = made[p]

    def z_stage(b, c):
        for k in range(1, L):
            xcopy(b, c, k).wait()
        total = ownf[c]
        for k in range(1, L):
            total = total + ra[b, c, k - 1].astype(jnp.float32)
        ownf[c] = total
        zg[b, c, a] = total.astype(jnp.bfloat16)
        for k in (1, 3, 2):
            ycopy(b, c, k).start()

    def finish(b, c):
        for k in range(1, Z):
            ycopy(b, c, k).wait()
        total = ownf[c, z]
        for k in range(1, Z):
            total = total + rz[b, c, k - 1].astype(jnp.float32)
        out[b, :, cols(c)] = total.astype(jnp.bfloat16)

    def give_back(b, n, one, two):
        pl.when(n < CHUNKS)(lambda: combine(b, n))
        pl.when((n >= one) & (n < CHUNKS + one))(lambda: z_stage(b, n - one))
        pl.when(n >= two)(lambda: finish(b, n - two))

    told = [
        remote(meta, metas.at[mine], ms.at[k], mr.at[k], device) for k, device in enumerate(mates)
    ]
    for copy in told:
        copy.start()

    def first(c, carry):
        z_send(0, c)
        return carry

    lax.fori_loop(0, CHUNKS, first, 0)

    def keep(c, carry):
        for b in range(2):
            kcopy(b, c).start()
        return carry

    lax.fori_loop(0, CHUNKS, keep, 0)

    batch_blocks = cache.shape[1]
    n_blocks = 2 * batch_blocks
    ring = blocks.shape[0]
    latent = mix.shape[2]

    def block_copy(n):
        slot = lax.rem(n, ring)
        return pltpu.make_async_copy(
            cache.at[n // batch_blocks, lax.rem(n, batch_blocks)], blocks.at[slot], cs.at[slot]
        )

    best[...] = jnp.full(best.shape, floor_value, jnp.float32)
    sums[...] = jnp.zeros_like(sums)
    mix[...] = jnp.zeros_like(mix)
    for n in range(ring - 1):
        block_copy(n).start()

    def attend(n):
        b, c = n // batch_blocks, lax.rem(n, batch_blocks)
        pl.when(n + ring - 1 < n_blocks)(lambda: block_copy(n + ring - 1).start())
        block_copy(n).wait()
        block = blocks[lax.rem(n, ring)]
        scores = lax.dot_general(
            ask[b], block, (((1,), (1,)), ((), ())), preferred_element_type=jnp.float32
        )
        scores = scores * score_scale
        head = lax.broadcasted_iota(jnp.int32, scores.shape, 0) // HEADS
        key = lax.broadcasted_iota(jnp.int32, scores.shape, 1)
        live = (head == breq[b, c]) & (key < blen[b, c])
        scores = jnp.where(live, scores, floor_value)
        before = best[b]
        now = jnp.maximum(before, jnp.max(scores, axis=1, keepdims=True))
        fade = jnp.exp(before - now)
        weights = jnp.where(live, jnp.exp(scores - now[:, 0:1]), 0.0)
        best[b] = now
        sums[b] = sums[b] * fade + jnp.sum(weights, axis=1, keepdims=True)
        mix[b] = mix[b] * fade[:, 0:1] + jnp.dot(
            weights.astype(jnp.bfloat16), block[:, :latent], preferred_element_type=jnp.float32
        )

    metas[mine] = meta[...]
    for copy in told:
        copy.wait()
    step = 256
    pairs = L * Z // 2
    tiles = rows // step

    def fill(n, carry):
        t, p = n // pairs, lax.rem(n, pairs)
        lane = lax.broadcasted_iota(jnp.int32, (16, 2 * tokens), 1)
        index = lax.broadcasted_iota(jnp.int32, (step, 2 * tokens), 0) + t * step + mine * rows
        index = index.astype(jnp.float32)
        for b in range(2):
            both = jnp.where(lane < tokens, metas[2 * p, b], metas[2 * p + 1, b])
            chosen = jnp.zeros(index.shape, jnp.float32)
            weight = jnp.zeros(index.shape, jnp.float32)
            for k in range(TOPK):
                hit = index == both[k : k + 1, :]
                chosen = jnp.where(hit, 1.0, chosen)
                weight = jnp.where(hit, both[8 + k : 9 + k, :], weight)
            at = pl.ds(pl.multiple_of(t * step, step), step)
            span = pl.ds(pl.multiple_of(p * 2 * tokens, 128), 2 * tokens)
            tab[b, at, span] = chosen.astype(jnp.bfloat16)
            wei[b, span, at] = weight.T.astype(jnp.bfloat16)
        return carry

    lax.fori_loop(0, tiles * pairs, fill, 0)

    per_chunk = -(-n_blocks // CHUNKS)

    def send_first(c, carry):
        g_send(0, c)

        @pl.when(c >= CHUNKS // 2)
        def _():
            z_send(1, 2 * c - CHUNKS)
            z_send(1, 2 * c - CHUNKS + 1)

        for u in range(per_chunk):
            n = c * per_chunk + u
            pl.when(n < n_blocks)(lambda: attend(n))
        pl.when(c > 0)(lambda: r_send(0, c - 1))
        return carry

    lax.fori_loop(0, CHUNKS, send_first, 0)
    r_send(0, CHUNKS - 1)
    lane = lax.broadcasted_iota(jnp.int32, best.shape, 2)
    stats[...] = jnp.where(lane == 0, best[...], sums[...]).reshape(stats.shape)
    parts[...] = mix[...].reshape(parts.shape).astype(jnp.bfloat16)
    shares = []
    for k, p in enumerate(inner_to):
        shares.append(remote(stats.at[p], got_stats.at[i], ss.at[k], sr.at[k], (g, p)))
        shares.append(remote(parts.at[p], got_parts.at[i], qs.at[k], qr.at[k], (g, p)))
    for copy in shares:
        copy.start()
    got_stats[i] = stats[i]
    got_parts[i] = parts[i]

    def gather_second(c, carry):
        g_send(1, c)
        return carry

    lax.fori_loop(0, CHUNKS, gather_second, 0)

    def early_second(c, carry):
        r_send(1, c)
        return carry

    lax.fori_loop(0, EARLY, early_second, 0)
    r_wait(0)

    def second(t, carry):
        pl.when(t + EARLY < CHUNKS)(lambda: r_send(1, t + EARLY))
        expert(0, t)
        return carry

    assert steps + EARLY >= CHUNKS
    lax.fori_loop(0, steps, second, 0)
    for copy in shares:
        copy.wait()
    joint = got_stats[0, :, 0:1]
    for p in range(1, n_inner):
        joint = jnp.maximum(joint, got_stats[p, :, 0:1])
    total = jnp.zeros_like(joint)
    summed = jnp.zeros(joined.shape, jnp.float32)
    for p in range(n_inner):
        scale = jnp.exp(got_stats[p, :, 0:1] - joint)
        total = total + got_stats[p, :, 1:2] * scale
        summed = summed + got_parts[p].astype(jnp.float32) * scale
    joined[...] = (summed / total).astype(jnp.bfloat16)
    spread = [remote(joined, whole.at[i], js.at[k], jr.at[k], (g, p)) for k, p in enumerate(inner_to)]
    spread.append(pltpu.make_async_copy(joined, whole.at[i], jl))
    for copy in spread:
        copy.start()
    b_wait(0)

    def ahead_of_third(n, carry):
        give_back(0, n, 1, 2)
        return carry

    lax.fori_loop(0, HEAD, ahead_of_third, 0)
    r_wait(1)


    def third(t, carry):
        expert(1, t)
        pl.when(t + HEAD < CHUNKS + 2)(lambda: give_back(0, t + HEAD, 1, 2))
        return carry

    lax.fori_loop(0, steps, third, 0)

    def rest(n, carry):
        give_back(0, n, 1, 2)
        return carry

    lax.fori_loop(min(steps + HEAD, CHUNKS + 2), CHUNKS + 2, rest, 0)
    b_wait(1)

    def fourth(n, carry):
        give_back(1, n, AFTER, 2 * AFTER + 1)
        return carry

    lax.fori_loop(0, CHUNKS + 2 * AFTER + 1, fourth, 0)

    def drain(s, carry):
        for b in range(2):
            for k in range(1, n_dst):
                bcopy(b, s, k).wait_send()
        return carry

    lax.fori_loop(0, slot_dev, drain, 0)
    for copy in spread:
        copy.wait()


def layer(tokens, route_weight, slots, w_in, w_out, queries, latent_cache, block_req, block_len):
    n_group, n_inner = lax.axis_size("group"), lax.axis_size("inner")
    batches, tok_count, width = tokens.shape
    requests, heads, feat_width = queries.shape[1:]
    asked = requests * heads
    share = batches * asked // n_inner
    assert heads == HEADS
    slot_dev = w_in.shape[0]
    length = n_group // 2
    assert n_inner == length * DEPTH and 2 * tok_count == 128
    per_slot = length * DEPTH * MOST
    n_dst = 2 * length
    rows = n_dst * slot_dev * per_slot
    count = length * DEPTH * tok_count
    chunk = width // CHUNKS
    part_ff = FF // (2 if n_dst * per_slot <= 384 else 8)
    order = jnp.arange(tok_count * TOPK, dtype=jnp.int32)
    same = (slots[:, :, None] == slots[:, None, :]) & (order[None, None, :] < order[None, :, None])
    position = jnp.sum(same.astype(jnp.int32), axis=2)
    device, local_slot = slots // slot_dev, slots % slot_dev
    dev_group, dev_inner = device // n_inner, device % n_inner
    dev_x, dev_core, dev_z, dev_y = dev_group // 2, dev_group % 2, dev_inner // length, dev_inner % length
    g, i = lax.axis_index("group"), lax.axis_index("inner")
    along_x = g % 2 == 0
    dev_a, dev_r = jnp.where(along_x, dev_x, dev_y), jnp.where(along_x, dev_y, dev_x)
    mine = jnp.where(along_x, g // 2, i % length) * DEPTH + i // length
    row = (dev_a * DEPTH + dev_z) * rows
    row = row + ((dev_r * 2 + dev_core) * slot_dev + local_slot) * per_slot + mine * MOST + position
    row = row.reshape(batches, tok_count, TOPK).transpose(0, 2, 1).astype(jnp.float32)
    weight = route_weight.transpose(0, 2, 1)
    meta = jnp.concatenate(
        [
            jnp.pad(row, ((0, 0), (0, 2), (0, 0)), constant_values=-1.0),
            jnp.pad(weight, ((0, 0), (0, 2), (0, 0))),
        ],
        axis=1,
    )
    meta = jnp.concatenate([meta, meta], axis=2)
    vmem, hbm = pl.BlockSpec(memory_space=pltpu.VMEM), pl.BlockSpec(memory_space=pl.ANY)
    sem = pltpu.SemaphoreType.DMA
    bf16, f32 = jnp.bfloat16, jnp.float32
    boxes = pltpu.VMEM((2, CHUNKS, n_dst, slot_dev, per_slot, chunk), bf16)
    return pl.pallas_call(
        partial(layer_kernel, length, n_inner),
        out_shape=(
            jax.ShapeDtypeStruct(tokens.shape, bf16),
            jax.ShapeDtypeStruct((n_inner, share, LAT), bf16),
        ),
        in_specs=[pl.BlockSpec(memory_space=pltpu.SMEM)] * 2 + [vmem] * 2 + [hbm] * 4,
        out_specs=(vmem, hbm),
        scratch_shapes=[
            pltpu.VMEM((2, CHUNKS, length, DEPTH, tok_count, chunk), bf16),
            boxes,
            pltpu.VMEM((2, CHUNKS, 2, length, slot_dev, per_slot, chunk), bf16),
            boxes,
            pltpu.VMEM((length * DEPTH,) + meta.shape, f32),
            pltpu.VMEM((2, rows, count), bf16),
            pltpu.VMEM((2, count, rows), bf16),
            pltpu.VMEM((CHUNKS, DEPTH, tok_count, chunk), f32),
            pltpu.VMEM((2, CHUNKS, length - 1, DEPTH, tok_count, chunk), bf16),
            pltpu.VMEM((2, CHUNKS, DEPTH - 1, tok_count, chunk), bf16),
            pltpu.VMEM((n_dst * per_slot, width), f32),
            pltpu.VMEM((2, 2, part_ff, width), bf16),
            pltpu.VMEM((2, part_ff, width), bf16),
            pltpu.VMEM((n_inner, share, 128), f32),
            pltpu.VMEM((n_inner, share, LAT), bf16),
            pltpu.VMEM((share, LAT), bf16),
            pltpu.VMEM((4,) + latent_cache.shape[2:], bf16),
            pltpu.VMEM((batches, asked, 128), f32),
            pltpu.VMEM((batches, asked, 128), f32),
            pltpu.VMEM((batches, asked, LAT), f32),
            pltpu.VMEM((n_inner, share, 128), f32),
            pltpu.VMEM((n_inner, share, LAT), bf16),
            sem((2, CHUNKS)),
            sem((4,)),
        ]
        + [sem((length * DEPTH,))] * 2
        + [sem((2, CHUNKS, DEPTH - 1))] * 2
        + [sem((2, CHUNKS, length - 1))] * 2
        + [sem((2, CHUNKS, n_dst - 1))] * 2
        + [sem((2, slot_dev, n_dst))] * 2
        + [sem((2, CHUNKS, length - 1))] * 2
        + [sem((2, CHUNKS, DEPTH - 1))] * 2
        + [sem((n_inner,))] * 6
        + [sem]
        + [sem((2,))] * 2,
        compiler_params=pltpu.CompilerParams(
            collective_id=1, has_side_effects=True, vmem_limit_bytes=62 * 2**20
        ),
        cost_estimate=pl.CostEstimate(
            flops=6 * batches * slot_dev * n_dst * per_slot * FF * width,
            bytes_accessed=6 * batches * slot_dev * FF * width,
            transcendentals=0,
        ),
        name="layer",
    )(
        block_req,
        block_len,
        meta,
        queries.reshape(batches, asked, feat_width),
        tokens,
        latent_cache,
        w_in.reshape(slot_dev, 2, FF, width),
        w_out,
    )


def local(
    tokens,
    route_weight,
    routes,
    replica,
    old_place,
    new_src,
    w_in,
    w_out,
    queries,
    latent_cache,
    block_req,
    block_len,
):
    slot_index = jnp.arange(old_place.shape[0], dtype=jnp.int32)
    keys = jnp.stack([replica_keys(old_place), replica_keys(table_lookup(new_src, old_place))])
    weight_slot = jnp.stack([slot_index, new_src])
    route_key = (routes * 2 + replica).reshape(2, -1)
    slots = jnp.sum(
        jnp.where(route_key[:, :, None] == keys[:, None, :], weight_slot[:, None, :], 0), axis=2
    )
    moe_out, attention = layer(
        tokens, route_weight, slots, w_in, w_out, queries, latent_cache, block_req, block_len
    )
    attention = attention.reshape(queries.shape[:3] + (LAT,))
    return (moe_out, attention)


def solution(mesh):
    in_specs = (
        P(None, ("group", "inner"), None),
        P(None, ("group", "inner"), None),
        P(None, ("group", "inner"), None),
        P(None, ("group", "inner"), None),
        P(),
        P(),
        P(("group", "inner"), None, None),
        P(("group", "inner"), None, None),
        P(None, "group", None, None),
        P(None, ("group", "inner"), None, None),
        P(None, ("group", "inner")),
        P(None, ("group", "inner")),
    )
    out_specs = (P(None, ("group", "inner"), None), P(None, "group", None, None))
    return jax.shard_map(local, mesh=mesh, in_specs=in_specs, out_specs=out_specs, check_vma=False)
```
